32 devices in a mesh: row: 2 (over x), col: 16 (over z, y, core).
Axes of the slice: x: 2, y: 2, z: 4, core: 2. Of those that a mesh axis runs over, the one named last changes fastest.
Arguments:
- tokens: bfloat16 [16384, 1024], P('col'), may hold values from -40 to 40
- segment_ids: int32 [16384], P('col'), may hold values from 0 to 127, as said below
- qkv_weight: bfloat16 [1, 1024, 3, 1024], P(None, 'col', None, 'row'), may hold values from -0.1875 to 0.1875
- attn_bias: float32 [1, 2, 1024], P(None, None, 'row'), may hold values from -3 to 3
- out_weight: bfloat16 [1, 1024, 1024], P(None, 'row', 'col'), may hold values from -0.1875 to 0.1875
- ffn_in: bfloat16 [1, 1024, 4096], P(None, 'col', 'row'), may hold values from -0.1875 to 0.1875
- ffn_bias: float32 [1, 4096], P(None, 'row'), may hold values from -3 to 3
- ffn_out: bfloat16 [1, 4096, 1024], P(None, 'row', 'col'), may hold values from -0.09375 to 0.09375
- norm_gain: float32 [1, 2, 1024], replicated, may hold values from 0.5 to 1.5
- shift: float32 [1, 4, 1024], replicated, may hold values from -3 to 3
- cross_weight: bfloat16 [2, 1024, 2, 1024], P(None, 'col', None, 'row'), may hold values from -0.1875 to 0.1875
- page_owner: int32 [1024, 1], P('col'), may hold values from 0 to 15; in each aligned block of 64 rows (0 to 63, 64 to 127, ...) at most 8 rows name the same one
- cache_base: int32 [16], replicated, may hold values from 0 to 15
Outputs:
- encoded: bfloat16 [16384, 1024], P('col', 'row')
- kv_cache: bfloat16 [2, 36864, 2, 1024], P(None, 'col', None, 'row')
The draws below stay inside these ranges and needn't reach their ends.
Inputs may be any that keep to these rules, and one draw needn't show every extreme that they name: `segment_ids`: each request's tokens are consecutive and lie within one block of 1024 tokens (those of one index of col); block b holds requests b * 8 to b * 8 + 7 in order, each of at most 512 tokens, and some request has exactly 512. `page_owner`: among the 64 pages of one index of col, at most 8 name the same owner.
All inputs are finite; a program needn't handle non-finite values.
Results may differ from the reference program's by a relative error of at most 0.019.
Values may be sent and summed in bfloat16 or wider, within the bound.
A program may use at most 128 MiB of HBM per device.

```python
import math
import jax
import jax.numpy as jnp
import numpy as np
from jax import lax

D = 1024
HEADS = 16
HDIM = 64
FF = 4096
LAYERS = 1
DEC = 2
TOK_C = 1024
SEGS_C = 8
MINLEN = 16
PAGE = 16
BASE_MAX = 16
MAXLEN = 512
TOKENS = 16384
PAGES_C = 64
PAGES = 1024
CAP = 8
OWN_PAGES = 144
GROUPS = 2
N_COL = 16


def draw_tokens(key, part):
    noise_key, column_key, row_key = jax.random.split(jax.random.fold_in(key, 11), 3)
    column = jnp.arange(D, dtype=jnp.float32) / D
    column_scale = jnp.exp(jnp.log(0.4) + jnp.log(8.0) * column + jax.random.uniform(column_key, (D,), minval=-0.3, maxval=0.3))
    row_scale = jnp.exp(jax.random.uniform(row_key, (TOKENS, 1), minval=jnp.log(0.3), maxval=jnp.log(3.0)))
    noise = jax.random.normal(noise_key, (TOKENS, D))
    return jnp.clip(noise * row_scale * column_scale, -40.0, 40.0).astype(jnp.bfloat16)


def draw_segment_ids(key, part):
    block_count = TOKENS // TOK_C
    flag_key, forced_key, long_key, weight_key = jax.random.split(jax.random.fold_in(key, 23), 4)
    long_flags = jax.random.randint(flag_key, (block_count,), 0, 2)
    forced = jax.random.randint(forced_key, (), 0, block_count)
    long_flags = jnp.where(jnp.arange(block_count) == forced, 1, long_flags)
    long_position = jax.random.randint(long_key, (block_count,), 0, SEGS_C)
    slot_range = jnp.arange(SEGS_C)[None, :]
    is_long = (slot_range == long_position[:, None]) & (long_flags[:, None] == 1)
    share_weights = jax.random.randint(weight_key, (block_count, SEGS_C), 8, 17)
    share_weights = jnp.where(is_long, 0, share_weights)
    base_lengths = jnp.where(is_long, MAXLEN, MINLEN)
    remaining = TOK_C - jnp.sum(base_lengths, axis=1, keepdims=True)
    shares = remaining * share_weights // jnp.sum(share_weights, axis=1, keepdims=True)
    leftover = remaining - jnp.sum(shares, axis=1, keepdims=True)
    fill_position = (long_position + 1) % SEGS_C
    shares = shares + jnp.where(slot_range == fill_position[:, None], leftover, 0)
    lengths = base_lengths + shares
    segment_ends = jnp.cumsum(lengths, axis=1)
    positions = jnp.arange(TOK_C)
    local_index = jnp.sum((positions[None, :, None] >= segment_ends[:, None, :]).astype(jnp.int32), axis=2)
    segment_index = local_index + jnp.arange(block_count)[:, None] * SEGS_C
    return segment_index.reshape(TOKENS).astype(jnp.int32)


def set_ends(drawn, key, smallest, top_value):
    extent = drawn.shape
    place = [jax.random.randint(jax.random.fold_in(key, axis), (), 0, extent[axis]) for axis in range(len(extent))]
    drawn = drawn.at[tuple(place)].set(smallest)
    longest = extent.index(max(extent))
    place[longest] = (place[longest] + 1) % extent[longest]
    return drawn.at[tuple(place)].set(top_value)


def level_of(stream_key, shape, cuts, low, top_value):
    factor_of = 1.0
    for axis_at, shards_of in cuts:
        steps = jax.random.uniform(jax.random.fold_in(jax.random.fold_in(stream_key, 6), axis_at), (shards_of,), jnp.float32, low / len(cuts), top_value / len(cuts))
        factor_of = factor_of * jnp.repeat(jnp.exp(steps), shape[axis_at] // shards_of).reshape((-1,) + (1,) * (len(shape) - 1 - axis_at))
    return factor_of


def assign_block(rng, own, number, rows, number_of, top, reach, slope):
    ranking = jax.random.permutation(rng, number_of)
    heavy_load, ordinary = load_shares(number_of, rows * top, reach, slope, True), load_shares(number_of, rows * top, reach, slope, False)
    places = jnp.arange(number_of)

    def named(sizes, offset_by):
        used = int((sizes > 0).sum())
        fixed = max(1, used // 4)
        moved = fixed + (places - fixed + offset_by * (used - fixed)) % max(1, number_of - fixed)
        return jnp.zeros((number_of,), jnp.int32).at[ranking[jnp.where(places < fixed, places, moved)]].set(jnp.asarray(sizes, jnp.int32))

    sizes = jnp.where(number % 4 == 0, named(heavy_load, number // 4), named(ordinary, number - number // 4 - 1))
    mixed = jax.random.permutation(jax.random.fold_in(own, 3), number_of)
    source_of, taker = mixed[0:number_of // 2 * 2:2], mixed[1:number_of // 2 * 2:2]
    margin = jnp.minimum(sizes[source_of] - 1, reach - sizes[taker]) // 2
    margin = jnp.where((source_of == ranking[0]) | (taker == ranking[0]) | (sizes[taker] == 0), 0, jnp.maximum(margin, 0))
    moved = jax.random.randint(jax.random.fold_in(own, 4), (number_of // 2,), 0, 1 << 20) % (margin + 1)
    sizes = sizes.at[source_of].add(-moved).at[taker].add(moved)
    members = jnp.searchsorted(jnp.cumsum(sizes), jnp.arange(rows * top), side="right").astype(jnp.int32)
    grid = members.reshape(top, rows).T
    grid = grid[jax.random.permutation(jax.random.fold_in(own, 1), rows)]
    offset_by = jax.random.randint(jax.random.fold_in(own, 2), (rows, 1), 0, top)
    return jnp.take_along_axis(grid, (jnp.arange(top)[None, :] + offset_by) % top, axis=1)


def load_shares(amount, total, bound, lean, full):
    loads = [(1 << 20) // math.isqrt(grade ** lean) + 1 for grade in range(1, amount + 1)]
    largest = bound if full else min(bound, max(-(-total // amount), total * loads[0] // sum(loads)))
    least = 1 if total - largest >= amount - 1 else 0
    given, spare = [largest] + [least] * (amount - 1), total - largest - least * (amount - 1)
    while spare > 0:
        candidates = [i for i in range(1, amount) if given[i] < largest] or [i for i in range(1, amount) if given[i] < bound]
        whole, left = sum([loads[i] for i in candidates]), spare
        for i in candidates:
            addition = min(bound - given[i], max(1, left * loads[i] // whole), spare)
            given[i] = given[i] + addition
            spare = spare - addition
    return np.array(given)


def gaussian(rng, extent, scale, limit, pieces=(), kind=jnp.bfloat16):
    gain = level_of(rng, extent, pieces, -0.22, 0.18) if pieces else 1.0
    entries = jax.random.normal(rng, extent, jnp.float32) * scale * gain
    return jnp.minimum(jnp.maximum(entries, -limit), limit).astype(kind)


def setup_inputs(seed: int = 0) -> dict:
    key_list = jax.random.split(jax.random.key(seed), 14)
    tokens = draw_tokens(jax.random.fold_in(key_list[13], 71), 0)
    segment_ids = draw_segment_ids(jax.random.fold_in(key_list[13], 71), 0)
    qkv_weight = gaussian(key_list[2], (LAYERS, D, 3, D), D ** -0.5, 0.1875, ((1, 16), (3, 2)))
    attn_bias = gaussian(key_list[3], (LAYERS, 2, D), 0.5, 3.0, ((2, 2),), jnp.float32)
    out_weight = gaussian(key_list[4], (LAYERS, D, D), D ** -0.5, 0.1875, ((1, 2), (2, 16)))
    ffn_in = gaussian(key_list[5], (LAYERS, D, FF), D ** -0.5, 0.1875, ((1, 16), (2, 2)))
    ffn_bias = gaussian(key_list[6], (LAYERS, FF), 0.5, 3.0, ((1, 2),), jnp.float32)
    ffn_out = gaussian(key_list[7], (LAYERS, FF, D), FF ** -0.5, 0.09375, ((1, 2), (2, 16)))
    norm_gain = jnp.clip(1.0 + 0.1 * jax.random.normal(key_list[8], (LAYERS, 2, D), jnp.float32), 0.5, 1.5)
    shift = gaussian(key_list[9], (LAYERS, 4, D), 0.5, 3.0, (), jnp.float32)
    cross_weight = gaussian(key_list[10], (DEC, D, 2, D), D ** -0.5, 0.1875, ((1, 16), (3, 2)))
    page_owner_keys = jax.random.split(jax.random.fold_in(key_list[11], 1), PAGES // PAGES_C)
    page_owner_turns = jax.random.permutation(jax.random.fold_in(key_list[11], 3), PAGES // PAGES_C)
    page_owner = jax.vmap(lambda own, number: assign_block(jax.random.fold_in(key_list[11], 2), own, number, PAGES_C, N_COL, 1, CAP, 2))(page_owner_keys, page_owner_turns).reshape((PAGES, 1))
    cache_base = set_ends(jax.random.randint(key_list[12], (N_COL,), 0, BASE_MAX), jax.random.fold_in(key_list[12], 1), 0, BASE_MAX - 1).astype(jnp.int32)
    return dict(tokens=tokens, segment_ids=segment_ids, qkv_weight=qkv_weight, attn_bias=attn_bias, out_weight=out_weight, ffn_in=ffn_in, ffn_bias=ffn_bias, ffn_out=ffn_out, norm_gain=norm_gain, shift=shift, cross_weight=cross_weight, page_owner=page_owner, cache_base=cache_base)


def layer_norm(summed, scaling_gain, offset_row):
    average = lax.optimization_barrier(jnp.mean(summed, axis=-1, keepdims=True))
    variance = lax.optimization_barrier(jnp.mean(summed * summed, axis=-1, keepdims=True)) - average * average
    return ((summed - average) * lax.rsqrt(variance + 1e-05) * scaling_gain + offset_row).astype(jnp.bfloat16)

def grouped_product(left, right):
    group_width = left.shape[1] // GROUPS
    running = jnp.zeros((left.shape[0], right.shape[1]), jnp.float32)
    for group_index in range(GROUPS):
        low = group_index * group_width
        product_term = jnp.dot(left[:, low:low + group_width], right[low:low + group_width], preferred_element_type=jnp.float32)
        rounded = lax.optimization_barrier(product_term.astype(jnp.bfloat16))
        running = running + rounded.astype(jnp.float32)
    return running

def attend_block(inputs):
    queries, key_rows, values, segment = inputs
    scores = jnp.einsum('qhd,khd->hqk', queries.astype(jnp.float32), key_rows.astype(jnp.float32))
    allowed = segment[:, None] == segment[None, :]
    scores = jnp.where(allowed[None], scores, -1e+30)
    highest = lax.optimization_barrier(jnp.max(scores, axis=2, keepdims=True))
    exponent = jnp.exp(scores - highest)
    probabilities = (exponent / lax.optimization_barrier(jnp.sum(exponent, axis=2, keepdims=True))).astype(jnp.bfloat16)
    return jnp.einsum('hqk,khd->qhd', probabilities.astype(jnp.float32), values.astype(jnp.float32)).astype(jnp.bfloat16)

def reference(tokens, segment_ids, qkv_weight, attn_bias, out_weight, ffn_in, ffn_bias, ffn_out, norm_gain, shift, cross_weight, page_owner, cache_base):
    current = tokens
    for layer_index in range(LAYERS):
        projected = jnp.dot(current, qkv_weight[layer_index].reshape(D, 3 * D), preferred_element_type=jnp.float32).reshape(TOKENS, 3, D)
        queries = ((projected[:, 0] + attn_bias[layer_index, 0]) * HDIM ** (-0.5)).astype(jnp.bfloat16)
        key_rows = projected[:, 1].astype(jnp.bfloat16)
        values = (projected[:, 2] + attn_bias[layer_index, 1]).astype(jnp.bfloat16)
        shaped = (N_COL, TOK_C, HEADS, HDIM)
        context = lax.map(attend_block, (queries.reshape(shaped), key_rows.reshape(shaped), values.reshape(shaped), segment_ids.reshape(N_COL, TOK_C)))
        context = context.reshape(TOKENS, D)
        attended = grouped_product(context, out_weight[layer_index])
        normed = layer_norm(current.astype(jnp.float32) + attended + shift[layer_index, 0], norm_gain[layer_index, 0], shift[layer_index, 1])
        hidden = jnp.dot(normed, ffn_in[layer_index], preferred_element_type=jnp.float32) + ffn_bias[layer_index]
        hidden = jax.nn.gelu(hidden, approximate=False).astype(jnp.bfloat16)
        fed = grouped_product(hidden, ffn_out[layer_index])
        current = layer_norm(normed.astype(jnp.float32) + fed + shift[layer_index, 2], norm_gain[layer_index, 1], shift[layer_index, 3])
    cross_list = []
    for layer_index in range(DEC):
        pairs = jnp.dot(current, cross_weight[layer_index].reshape(D, 2 * D), preferred_element_type=jnp.float32).astype(jnp.bfloat16)
        cross_list.append(pairs.reshape(PAGES, PAGE * 2 * D))
    page_rows = jnp.stack(cross_list)
    owners = page_owner[:, 0].astype(jnp.int32)
    onehot = (owners[:, None] == jnp.arange(N_COL, dtype=jnp.int32)[None, :]).astype(jnp.int32)
    before = jnp.cumsum(onehot, axis=0) - onehot
    slot_index = lax.optimization_barrier(jnp.sum(onehot * (before + cache_base[None, :].astype(jnp.int32)), axis=1))
    destination = (owners * OWN_PAGES + slot_index).astype(jnp.int32)
    cache_rows = jnp.zeros((DEC, N_COL * OWN_PAGES, PAGE * 2 * D), jnp.bfloat16).at[:, destination].set(page_rows)
    return (current, cache_rows.reshape(DEC, N_COL * OWN_PAGES * PAGE, 2, D))
```

```python
import functools

import jax
import jax.numpy as jnp
from jax import lax
from jax.experimental import pallas as pl
from jax.experimental.pallas import tpu as pltpu
from jax.sharding import PartitionSpec as P

HDIM = 64
PAGE = 16
BASE_MAX = 16
EPSILON = 1e-05
NEGATIVE = -1e30
CHUNKS = 2
MIB = 1 << 20
MESH = pl.DeviceIdType.MESH


def attend_kernel(
    x_ref, w_ref, bias_ref, seg_col_ref, seg_row_ref, out_ref, q_ref, k_ref, v_ref, *, q_rows
):
    x = x_ref[...]
    q = jnp.dot(x, w_ref[0], preferred_element_type=jnp.float32)
    q_ref[...] = ((q + bias_ref[0:1]) * HDIM ** (-0.5)).astype(jnp.bfloat16)
    k = jnp.dot(x, w_ref[1], preferred_element_type=jnp.float32)
    k_ref[...] = k.astype(jnp.bfloat16)
    v = jnp.dot(x, w_ref[2], preferred_element_type=jnp.float32)
    v_ref[...] = (v + bias_ref[1:2]).astype(jnp.bfloat16)
    tokens, width = q_ref.shape

    def block(i, _):
        rows = pl.ds(pl.multiple_of(i * q_rows, q_rows), q_rows)
        allowed = seg_col_ref[rows, :] == seg_row_ref[...]
        parts = []
        for h in range(width // HDIM):
            cols = slice(h * HDIM, (h + 1) * HDIM)
            scores = lax.dot_general(
                q_ref[rows, cols],
                k_ref[:, cols],
                (((1,), (1,)), ((), ())),
                preferred_element_type=jnp.float32,
            )
            scores = jnp.where(allowed, scores, NEGATIVE)
            highest = jnp.max(scores, axis=1, keepdims=True)
            exponent = jnp.exp(scores - highest)
            total = jnp.sum(exponent, axis=1, keepdims=True)
            mixed = jnp.dot(
                exponent.astype(jnp.bfloat16), v_ref[:, cols], preferred_element_type=jnp.float32
            )
            parts.append(mixed / total)
        out_ref[rows, :] = jnp.concatenate(parts, axis=1).astype(jnp.bfloat16)
        return 0

    lax.fori_loop(0, tokens // q_rows, block, 0)


def attention(tokens, weight, bias, segment):
    count, depth = tokens.shape
    width = weight.shape[2]
    step = 256
    return pl.pallas_call(
        functools.partial(attend_kernel, q_rows=256),
        grid=(width // step,),
        in_specs=[
            pl.BlockSpec((count, depth), lambda i: (0, 0)),
            pl.BlockSpec((3, depth, step), lambda i: (0, 0, i)),
            pl.BlockSpec((2, step), lambda i: (0, i)),
            pl.BlockSpec((count, 1), lambda i: (0, 0)),
            pl.BlockSpec((1, count), lambda i: (0, 0)),
        ],
        out_specs=pl.BlockSpec((count, step), lambda i: (0, i)),
        out_shape=jax.ShapeDtypeStruct((count, width), jnp.bfloat16),
        scratch_shapes=[pltpu.VMEM((count, step), jnp.bfloat16)] * 3,
        compiler_params=pltpu.CompilerParams(vmem_limit_bytes=40 * MIB),
        cost_estimate=pl.CostEstimate(
            flops=40 * 10**9, bytes_accessed=6 * MIB, transcendentals=8 * MIB
        ),
        name="attention",
    )(tokens, weight, bias, segment[:, None], segment[None, :])


def dispatch_kernel(n, out_ref, got_ref, local_sem, send_sem, recv_sem, send2_sem, recv2_sem):
    me, side = lax.axis_index("col"), lax.axis_index("row")
    other = 1 - side
    barrier = pltpu.get_barrier_semaphore()
    for k in range(1, n):
        pl.semaphore_signal(
            barrier, inc=1, device_id=(side, lax.rem(me + k, n)), device_id_type=MESH
        )
    pl.semaphore_signal(barrier, inc=1, device_id=(other, me), device_id_type=MESH)
    pl.semaphore_wait(barrier, n)

    def first(k):
        target = lax.rem(me + k, n)
        return pltpu.make_async_remote_copy(
            src_ref=out_ref.at[target],
            dst_ref=got_ref.at[side, me],
            send_sem=send_sem.at[k],
            recv_sem=recv_sem.at[k],
            device_id=(side, target),
            device_id_type=MESH,
        )

    def second(k, source):
        return pltpu.make_async_remote_copy(
            src_ref=source,
            dst_ref=got_ref.at[side, lax.rem(me + n - k, n)],
            send_sem=send2_sem.at[k],
            recv_sem=recv2_sem.at[k],
            device_id=(other, me),
            device_id_type=MESH,
        )

    firsts = [first(k) for k in range(1, n)]
    for copy in firsts:
        copy.start()
    own = pltpu.make_async_copy(out_ref.at[me], got_ref.at[side, me], local_sem)
    own.start()
    seconds = [second(0, out_ref.at[me])]
    seconds[0].start()
    for k in range(1, n):
        firsts[k - 1].wait_recv()
        copy = second(k, got_ref.at[side, lax.rem(me + n - k, n)])
        copy.start()
        seconds.append(copy)
    own.wait()
    for copy in firsts:
        copy.wait_send()
    for copy in seconds:
        copy.wait()


def dispatch(outgoing):
    n, rows, width = outgoing.shape
    return pl.pallas_call(
        functools.partial(dispatch_kernel, n),
        in_specs=[pl.BlockSpec(memory_space=pl.ANY)],
        out_specs=pl.BlockSpec(memory_space=pl.ANY),
        out_shape=jax.ShapeDtypeStruct((2, n, rows, width), outgoing.dtype),
        scratch_shapes=[pltpu.SemaphoreType.DMA(())] + [pltpu.SemaphoreType.DMA((n,))] * 4,
        compiler_params=pltpu.CompilerParams(collective_id=1, has_side_effects=True),
        name="dispatch",
    )(outgoing)


def cache_kernel(index_ref, got_ref, w_ref, out_ref, x_ref, *, pages):
    base = pl.program_id(0) * pages
    half = got_ref.shape[2]
    for j in range(pages):
        at = index_ref[base + j]
        rows = pl.ds(pl.multiple_of(jnp.maximum(at, 0) * PAGE, PAGE), PAGE)
        for s in range(2):
            page = got_ref[s, rows, :]
            page = jnp.where(at >= 0, page, jnp.zeros_like(page))
            x_ref[j * PAGE : (j + 1) * PAGE, s * half : (s + 1) * half] = page
    x = x_ref[...]
    for d in range(w_ref.shape[0]):
        for k in range(2):
            out_ref[d, k] = jnp.dot(x, w_ref[d, k], preferred_element_type=jnp.float32).astype(
                jnp.bfloat16
            )


def fill_cache(index, got, weight, pages):
    own_pages = index.shape[0]
    layers, _, depth, width = weight.shape
    return pl.pallas_call(
        functools.partial(cache_kernel, pages=pages),
        grid_spec=pltpu.PrefetchScalarGridSpec(
            num_scalar_prefetch=1,
            grid=(own_pages // pages,),
            in_specs=[
                pl.BlockSpec(got.shape, lambda i, s: (0, 0, 0)),
                pl.BlockSpec(weight.shape, lambda i, s: (0, 0, 0, 0)),
            ],
            out_specs=pl.BlockSpec((layers, 2, pages * PAGE, width), lambda i, s: (0, 0, i, 0)),
            scratch_shapes=[pltpu.VMEM((pages * PAGE, depth), jnp.bfloat16)],
        ),
        out_shape=jax.ShapeDtypeStruct((layers, 2, own_pages * PAGE, width), jnp.bfloat16),
        compiler_params=pltpu.CompilerParams(vmem_limit_bytes=40 * MIB),
        cost_estimate=pl.CostEstimate(
            flops=10**10, bytes_accessed=18 * MIB, transcendentals=0
        ),
        name="fill_cache",
    )(index, got, weight)


def settle(partial_value, residual, shift_first, gain_row, shift_second):
    mine = partial_value.astype(jnp.bfloat16)
    theirs = lax.ppermute(mine, "row", [(0, 1), (1, 0)])
    summed = (
        residual.astype(jnp.float32)
        + (mine.astype(jnp.float32) + theirs.astype(jnp.float32))
        + shift_first
    )
    average = jnp.mean(summed, axis=1, keepdims=True)
    variance = jnp.mean(summed * summed, axis=1, keepdims=True) - average * average
    return (
        (summed - average) * lax.rsqrt(variance + EPSILON) * gain_row + shift_second
    ).astype(jnp.bfloat16)


def times_transposed(left, right):
    return lax.dot_general(
        left, right, (((1,), (1,)), ((), ())), preferred_element_type=jnp.float32
    )


def per_device(
    tokens,
    segment_ids,
    qkv_weight,
    attn_bias,
    out_weight,
    ffn_in,
    ffn_bias,
    ffn_out,
    norm_gain,
    shift,
    cross_weight,
    page_owner,
    cache_base,
):
    token_count = tokens.shape[0]
    n, me = lax.axis_size("col"), lax.axis_index("col")

    def gather(value, axis):
        return lax.all_gather(value, "col", axis=axis, tiled=True)

    w_qkv = gather(qkv_weight[0].transpose(1, 0, 2), 1)
    w_out = gather(out_weight[0].T, 0)
    w_in = gather(ffn_in[0], 0)
    w_down = gather(ffn_out[0].T, 0)
    w_cross = gather(cross_weight.transpose(0, 2, 1, 3), 2)
    all_owners = lax.all_gather(page_owner[:, 0], "col")

    page_count = page_owner.shape[0]
    capacity = max(2, (2 * page_count + n - 1) // n)
    owner_ids = jnp.arange(n, dtype=jnp.int32)
    owners = page_owner[:, 0]
    onehot = (owners[:, None] == owner_ids[None, :]).astype(jnp.int32)
    local_rank = jnp.sum((jnp.cumsum(onehot, axis=0) - onehot) * onehot, axis=1)
    target = owners * capacity + local_rank
    token_target = (
        target[:, None] * PAGE + jnp.arange(PAGE, dtype=jnp.int32)[None, :]
    ).reshape(token_count)
    chosen = (
        jnp.arange(n * capacity * PAGE, dtype=jnp.int32)[:, None] == token_target[None, :]
    ).astype(jnp.bfloat16)
    received = jnp.sum((all_owners == me).astype(jnp.int32), axis=1)
    earlier = jnp.cumsum(received) - received
    own_base = jnp.sum(jnp.where(owner_ids == me, cache_base, 0))
    place_ids = jnp.arange(capacity, dtype=jnp.int32)
    slots = jnp.where(
        place_ids[None, :] < received[:, None],
        own_base + earlier[:, None] + place_ids[None, :],
        -1,
    ).reshape(n * capacity)
    own_pages = BASE_MAX + capacity * n
    hits = jnp.arange(own_pages, dtype=jnp.int32)[:, None] == slots[None, :]
    page_at = jnp.max(
        jnp.where(hits, jnp.arange(n * capacity, dtype=jnp.int32)[None, :], -1), axis=1
    )

    context = attention(tokens, w_qkv, attn_bias[0], segment_ids)
    rows = token_count // CHUNKS
    encoded = []
    for c in range(CHUNKS):
        part = slice(c * rows, (c + 1) * rows)
        normed = settle(
            times_transposed(context[part], w_out),
            tokens[part],
            shift[0, 0],
            norm_gain[0, 0],
            shift[0, 1],
        )
        hidden = jnp.dot(normed, w_in, preferred_element_type=jnp.float32)
        hidden = jax.nn.gelu(hidden + ffn_bias[0], approximate=False).astype(jnp.bfloat16)
        encoded.append(
            settle(
                times_transposed(hidden, w_down),
                normed,
                shift[0, 2],
                norm_gain[0, 1],
                shift[0, 3],
            )
        )
    width = cross_weight.shape[3]
    own_part = lax.dynamic_slice_in_dim(
        jnp.concatenate(encoded, axis=0), lax.axis_index("row") * width, width, 1
    )
    outgoing = jnp.dot(chosen, own_part, preferred_element_type=jnp.float32)
    outgoing = outgoing.astype(jnp.bfloat16).reshape(n, capacity * PAGE, width)
    arrived = dispatch(outgoing).reshape(2, n * capacity * PAGE, width)
    pages = 16 if own_pages % 16 == 0 else own_pages
    cache = fill_cache(page_at, arrived, w_cross, pages)
    return (own_part, cache.transpose(0, 2, 1, 3))


def solution(mesh):
    return jax.shard_map(
        per_device,
        mesh=mesh,
        in_specs=(
            P("col", None),
            P("col"),
            P(None, "col", None, "row"),
            P(None, None, "row"),
            P(None, "row", "col"),
            P(None, "col", "row"),
            P(None, "row"),
            P(None, "row", "col"),
            P(),
            P(),
            P(None, "col", None, "row"),
            P("col", None),
            P(),
        ),
        out_specs=(P("col", "row"), P(None, "col", None, "row")),
        check_vma=False,
    )
```

```python
import functools

import jax
import jax.numpy as jnp
from jax import lax
from jax.experimental import pallas as pl
from jax.experimental.pallas import tpu as pltpu
from jax.sharding import PartitionSpec as P

HDIM = 64
PAGE = 16
BASE_MAX = 16
EPSILON = 1e-05
NEGATIVE = -1e30
CHUNKS = 4
MIB = 1 << 20
MESH = pl.DeviceIdType.MESH


def project_kernel(x_ref, w_ref, bias_ref, scale_ref, out_ref):
    sums = jnp.dot(x_ref[...], w_ref[0], preferred_element_type=jnp.float32)
    out_ref[0] = ((sums + bias_ref[0]) * scale_ref[0]).astype(jnp.bfloat16)


def project(tokens, weight, bias, scale):
    count, depth = tokens.shape
    width = weight.shape[2]
    return pl.pallas_call(
        project_kernel,
        grid=(3,),
        in_specs=[
            pl.BlockSpec((count, depth), lambda i: (0, 0)),
            pl.BlockSpec((1, depth, width), lambda i: (i, 0, 0)),
            pl.BlockSpec((1, 1, width), lambda i: (i, 0, 0)),
            pl.BlockSpec((1, 1, width), lambda i: (i, 0, 0)),
        ],
        out_specs=pl.BlockSpec((1, count, width), lambda i: (i, 0, 0)),
        out_shape=jax.ShapeDtypeStruct((3, count, width), jnp.bfloat16),
        compiler_params=pltpu.CompilerParams(vmem_limit_bytes=40 * MIB),
        cost_estimate=pl.CostEstimate(
            flops=5 * 10**9, bytes_accessed=8 * MIB, transcendentals=0
        ),
        name="project",
    )(tokens, weight, bias, scale)


def attend_kernel(q_ref, k_ref, v_ref, seg_col_ref, seg_row_ref, out_ref):
    allowed = seg_col_ref[...] == seg_row_ref[...]
    parts = []
    for h in range(q_ref.shape[2] // HDIM):
        cols = slice(h * HDIM, (h + 1) * HDIM)
        scores = lax.dot_general(
            q_ref[0, :, cols],
            k_ref[0, :, cols],
            (((1,), (1,)), ((), ())),
            preferred_element_type=jnp.float32,
        )
        scores = jnp.where(allowed, scores, NEGATIVE)
        highest = jnp.max(scores, axis=1, keepdims=True)
        exponent = jnp.exp(scores - highest)
        total = jnp.sum(exponent, axis=1, keepdims=True)
        mixed = jnp.dot(
            exponent.astype(jnp.bfloat16), v_ref[0, :, cols], preferred_element_type=jnp.float32
        )
        parts.append(mixed / total)
    out_ref[...] = jnp.concatenate(parts, axis=1).astype(jnp.bfloat16)


def attention(qkv, seg_col, seg_row, chunk, rows):
    _, count, width = qkv.shape
    step = 256
    return pl.pallas_call(
        attend_kernel,
        grid=(width // step,),
        in_specs=[
            pl.BlockSpec((1, rows, step), lambda i: (0, chunk, i)),
            pl.BlockSpec((1, count, step), lambda i: (1, 0, i)),
            pl.BlockSpec((1, count, step), lambda i: (2, 0, i)),
            pl.BlockSpec((rows, 1), lambda i: (chunk, 0)),
            pl.BlockSpec((1, count), lambda i: (0, 0)),
        ],
        out_specs=pl.BlockSpec((rows, step), lambda i: (0, i)),
        out_shape=jax.ShapeDtypeStruct((rows, width), jnp.bfloat16),
        compiler_params=pltpu.CompilerParams(vmem_limit_bytes=40 * MIB),
        cost_estimate=pl.CostEstimate(
            flops=5 * 10**9, bytes_accessed=3 * MIB, transcendentals=2 * MIB
        ),
        name="attention",
    )(qkv, qkv, qkv, seg_col, seg_row)


def feed_kernel(
    side_ref, mine_ref, theirs_ref, x_ref, vec_ref, w_ref, bias_ref,
    *rest,
):
    *part_refs, half_ref, normed_ref, sum_ref = rest
    step = pl.program_id(0)
    width = half_ref.shape[1]
    count = len(part_refs)

    def columns(at):
        at = at % count
        return slice(at * width, (at + 1) * width)

    @pl.when(step == 0)
    def _():
        summed = (
            x_ref[...].astype(jnp.float32)
            + (mine_ref[...].astype(jnp.float32) + theirs_ref[...].astype(jnp.float32))
            + vec_ref[0:1]
        )
        average = jnp.mean(summed, axis=1, keepdims=True)
        variance = jnp.mean(summed * summed, axis=1, keepdims=True) - average * average
        normed = (summed - average) * lax.rsqrt(variance + EPSILON) * vec_ref[1:2] + vec_ref[2:3]
        normed_ref[...] = normed.astype(jnp.bfloat16)
        sum_ref[...] = jnp.zeros_like(sum_ref)

        for side in range(count):

            @pl.when(side_ref[0] == side)
            def _():
                half_ref[...] = normed_ref[:, columns(side)]

    hidden = jnp.dot(normed_ref[...], w_ref[0], preferred_element_type=jnp.float32)
    hidden = hidden + bias_ref[...]
    hidden = (0.5 * hidden * (1.0 + lax.erf(hidden * 0.5**0.5))).astype(jnp.bfloat16)
    sum_ref[...] += lax.dot_general(
        hidden, w_ref[1], (((1,), (1,)), ((), ())), preferred_element_type=jnp.float32
    )

    @pl.when(step == pl.num_programs(0) - 1)
    def _():
        for side in range(count):

            @pl.when(side_ref[0] == side)
            def _():
                for k, part_ref in enumerate(part_refs):
                    part_ref[...] = sum_ref[:, columns(side + k)].astype(jnp.bfloat16)


def feed(side, mine, theirs, tokens, chunk, vectors, weight, bias):
    rows, depth = mine.shape
    count = lax.axis_size("row")
    width = depth // count
    units = weight.shape[2]
    step = 512
    whole = pl.BlockSpec((rows, depth), lambda i, s: (0, 0))
    half = pl.BlockSpec((rows, width), lambda i, s: (0, 0))
    return pl.pallas_call(
        feed_kernel,
        grid_spec=pltpu.PrefetchScalarGridSpec(
            num_scalar_prefetch=1,
            grid=(units // step,),
            in_specs=[
                whole,
                whole,
                pl.BlockSpec((rows, depth), lambda i, s: (chunk, 0)),
                pl.BlockSpec((3, depth), lambda i, s: (0, 0)),
                pl.BlockSpec((2, depth, step), lambda i, s: (0, 0, i)),
                pl.BlockSpec((1, step), lambda i, s: (0, i)),
            ],
            out_specs=[half] * (count + 1),
            scratch_shapes=[
                pltpu.VMEM((rows, depth), jnp.bfloat16),
                pltpu.VMEM((rows, depth), jnp.float32),
            ],
        ),
        out_shape=[jax.ShapeDtypeStruct((rows, width), jnp.bfloat16)] * (count + 1),
        compiler_params=pltpu.CompilerParams(vmem_limit_bytes=40 * MIB),
        cost_estimate=pl.CostEstimate(
            flops=8 * 10**9, bytes_accessed=10 * MIB, transcendentals=rows * units
        ),
        name="feed",
    )(side, mine, theirs, tokens, vectors, weight, bias)


def dispatch_kernel(
    n, sides, out_ref, got_ref, local_sem, send_sem, recv_sem, send2_sem, recv2_sem
):
    me, side = lax.axis_index("col"), lax.axis_index("row")
    barrier = pltpu.get_barrier_semaphore()
    for k in range(1, n):
        pl.semaphore_signal(
            barrier, inc=1, device_id=(side, lax.rem(me + k, n)), device_id_type=MESH
        )
    for j in range(1, sides):
        pl.semaphore_signal(
            barrier, inc=1, device_id=(lax.rem(side + j, sides), me), device_id_type=MESH
        )
    pl.semaphore_wait(barrier, n - 1 + sides - 1)

    def first(k):
        target = lax.rem(me + k, n)
        return pltpu.make_async_remote_copy(
            src_ref=out_ref.at[target],
            dst_ref=got_ref.at[side, me],
            send_sem=send_sem.at[k],
            recv_sem=recv_sem.at[k],
            device_id=(side, target),
            device_id_type=MESH,
        )

    def second(j, k, source):
        return pltpu.make_async_remote_copy(
            src_ref=source,
            dst_ref=got_ref.at[side, lax.rem(me + n - k, n)],
            send_sem=send2_sem.at[j, k],
            recv_sem=recv2_sem.at[j, k],
            device_id=(lax.rem(side + j, sides), me),
            device_id_type=MESH,
        )

    firsts = [first(k) for k in range(1, n)]
    for copy in firsts:
        copy.start()
    own = pltpu.make_async_copy(out_ref.at[me], got_ref.at[side, me], local_sem)
    own.start()
    seconds = [second(j, 0, out_ref.at[me]) for j in range(1, sides)]
    for copy in seconds:
        copy.start()
    for k in range(1, n):
        firsts[k - 1].wait_recv()
        for j in range(1, sides):
            copy = second(j, k, got_ref.at[side, lax.rem(me + n - k, n)])
            copy.start()
            seconds.append(copy)
    own.wait()
    for copy in firsts:
        copy.wait_send()
    for copy in seconds:
        copy.wait()


def dispatch(outgoing):
    n, rows, width = outgoing.shape
    sides = lax.axis_size("row")
    return pl.pallas_call(
        functools.partial(dispatch_kernel, n, sides),
        in_specs=[pl.BlockSpec(memory_space=pl.ANY)],
        out_specs=pl.BlockSpec(memory_space=pl.ANY),
        out_shape=jax.ShapeDtypeStruct((sides, n, rows, width), outgoing.dtype),
        scratch_shapes=[pltpu.SemaphoreType.DMA(())]
        + [pltpu.SemaphoreType.DMA((n,))] * 2
        + [pltpu.SemaphoreType.DMA((sides, n))] * 2,
        compiler_params=pltpu.CompilerParams(collective_id=1, has_side_effects=True),
        name="dispatch",
    )(outgoing)


def cache_kernel(index_ref, got_ref, w_ref, out_ref, x_ref, *, pages):
    base = pl.program_id(0) * pages
    half = got_ref.shape[2]
    for j in range(pages):
        at = index_ref[base + j]
        rows = pl.ds(pl.multiple_of(jnp.maximum(at, 0) * PAGE, PAGE), PAGE)
        for s in range(got_ref.shape[0]):
            page = got_ref[s, rows, :]
            page = jnp.where(at >= 0, page, jnp.zeros_like(page))
            x_ref[j * PAGE : (j + 1) * PAGE, s * half : (s + 1) * half] = page
    x = x_ref[...]
    for d in range(w_ref.shape[0]):
        pair = [
            jnp.dot(x, w_ref[d, k], preferred_element_type=jnp.float32).astype(jnp.bfloat16)
            for k in range(2)
        ]
        out_ref[d] = jnp.stack(pair, axis=1)


def fill_cache(index, got, weight, pages):
    own_pages = index.shape[0]
    layers, _, depth, width = weight.shape
    return pl.pallas_call(
        functools.partial(cache_kernel, pages=pages),
        grid_spec=pltpu.PrefetchScalarGridSpec(
            num_scalar_prefetch=1,
            grid=(own_pages // pages,),
            in_specs=[
                pl.BlockSpec(got.shape, lambda i, s: (0, 0, 0)),
                pl.BlockSpec(weight.shape, lambda i, s: (0, 0, 0, 0)),
            ],
            out_specs=pl.BlockSpec((layers, pages * PAGE, 2, width), lambda i, s: (0, i, 0, 0)),
            scratch_shapes=[pltpu.VMEM((pages * PAGE, depth), jnp.bfloat16)],
        ),
        out_shape=jax.ShapeDtypeStruct((layers, own_pages * PAGE, 2, width), jnp.bfloat16),
        compiler_params=pltpu.CompilerParams(vmem_limit_bytes=40 * MIB),
        cost_estimate=pl.CostEstimate(
            flops=10**10, bytes_accessed=18 * MIB, transcendentals=0
        ),
        name="fill_cache",
    )(index, got, weight)


def send(value, step):
    count = lax.axis_size("row")
    return lax.ppermute(value, "row", [(i, (i + step) % count) for i in range(count)])


def from_others(values):
    got = [send(value, k + 1) for k, value in enumerate(values)]
    if len(got) == 1:
        return got[0]
    return sum(value.astype(jnp.float32) for value in got)


def times_transposed(left, right):
    return lax.dot_general(
        left, right, (((1,), (1,)), ((), ())), preferred_element_type=jnp.float32
    )


def per_device(
    tokens,
    segment_ids,
    qkv_weight,
    attn_bias,
    out_weight,
    ffn_in,
    ffn_bias,
    ffn_out,
    norm_gain,
    shift,
    cross_weight,
    page_owner,
    cache_base,
):
    token_count = tokens.shape[0]
    n, me = lax.axis_size("col"), lax.axis_index("col")

    def gather(value, axis):
        return lax.all_gather(value, "col", axis=axis, tiled=True)

    w_first = gather(
        jnp.concatenate([qkv_weight[0].transpose(1, 0, 2), out_weight.transpose(0, 2, 1)]), 1
    )
    w_ffn = gather(jnp.concatenate([ffn_in, ffn_out.transpose(0, 2, 1)]), 1)
    w_cross = gather(cross_weight.transpose(0, 2, 1, 3), 2)
    all_owners = lax.all_gather(page_owner[:, 0], "col")

    page_count = page_owner.shape[0]
    capacity = max(2, (2 * page_count + n - 1) // n)
    owner_ids = jnp.arange(n, dtype=jnp.int32)
    owners = page_owner[:, 0]
    onehot = (owners[:, None] == owner_ids[None, :]).astype(jnp.int32)
    local_rank = jnp.sum((jnp.cumsum(onehot, axis=0) - onehot) * onehot, axis=1)
    target = owners * capacity + local_rank
    token_target = (
        target[:, None] * PAGE + jnp.arange(PAGE, dtype=jnp.int32)[None, :]
    ).reshape(token_count)
    received = jnp.sum((all_owners == me).astype(jnp.int32), axis=1)
    earlier = jnp.cumsum(received) - received
    own_base = jnp.sum(jnp.where(owner_ids == me, cache_base, 0))
    place_ids = jnp.arange(capacity, dtype=jnp.int32)
    slots = jnp.where(
        place_ids[None, :] < received[:, None],
        own_base + earlier[:, None] + place_ids[None, :],
        -1,
    ).reshape(n * capacity)
    own_pages = BASE_MAX + capacity * n
    hits = jnp.arange(own_pages, dtype=jnp.int32)[:, None] == slots[None, :]
    page_at = jnp.max(
        jnp.where(hits, jnp.arange(n * capacity, dtype=jnp.int32)[None, :], -1), axis=1
    )

    page_at, token_target, tokens = lax.optimization_barrier((page_at, token_target, tokens))
    width = cross_weight.shape[3]
    side = lax.axis_index("row")
    others = lax.axis_size("row") - 1
    bias = jnp.stack([attn_bias[0, 0], jnp.zeros_like(attn_bias[0, 0]), attn_bias[0, 1]])
    scale = jnp.array([HDIM ** (-0.5), 1.0, 1.0], jnp.float32)[:, None, None]
    scale = jnp.broadcast_to(scale, (3, 1, bias.shape[1]))
    qkv = project(tokens, w_first, bias[:, None, :], scale)
    w_out = w_first[3]
    vectors = jnp.stack([shift[0, 0], norm_gain[0, 0], shift[0, 1]])
    rows = token_count // CHUNKS
    seg_col, seg_row = segment_ids[:, None], segment_ids[None, :]
    partials = []
    for c in range(CHUNKS):
        context = attention(qkv, seg_col, seg_row, c, rows)
        mine = times_transposed(context, w_out).astype(jnp.bfloat16)
        partials.append((mine, from_others([mine] * others)))
    kept, taken, halves = [], [], []
    for c, (mine, theirs) in enumerate(partials):
        keep, *sends, half = feed(
            side.reshape(1), mine, theirs, tokens, c, vectors, w_ffn, ffn_bias
        )
        kept.append(keep)
        taken.append(from_others(sends))
        halves.append(half)

    def own(row):
        return lax.dynamic_slice_in_dim(row, side * width, width, 0)

    summed = (
        jnp.concatenate(halves).astype(jnp.float32)
        + (jnp.concatenate(kept).astype(jnp.float32) + jnp.concatenate(taken).astype(jnp.float32))
        + own(shift[0, 2])
    )
    sums = jnp.stack([jnp.sum(summed, axis=1), jnp.sum(summed * summed, axis=1)])
    moments = (sums + from_others([sums] * others)) / tokens.shape[1]
    average = moments[0][:, None]
    variance = moments[1][:, None] - average * average
    own_part = (
        (summed - average) * lax.rsqrt(variance + EPSILON) * own(norm_gain[0, 1])
        + own(shift[0, 3])
    ).astype(jnp.bfloat16)
    chosen = (
        jnp.arange(n * capacity * PAGE, dtype=jnp.int32)[:, None] == token_target[None, :]
    ).astype(jnp.bfloat16)
    outgoing = jnp.dot(chosen, own_part, preferred_element_type=jnp.float32)
    outgoing = outgoing.astype(jnp.bfloat16).reshape(n, capacity * PAGE, width)
    arrived = dispatch(outgoing).reshape(others + 1, n * capacity * PAGE, width)
    pages = 16 if own_pages % 16 == 0 else own_pages
    cache = fill_cache(page_at, arrived, w_cross, pages)
    return (own_part, cache)


def solution(mesh):
    return jax.shard_map(
        per_device,
        mesh=mesh,
        in_specs=(
            P("col", None),
            P("col"),
            P(None, "col", None, "row"),
            P(None, None, "row"),
            P(None, "row", "col"),
            P(None, "col", "row"),
            P(None, "row"),
            P(None, "row", "col"),
            P(),
            P(),
            P(None, "col", None, "row"),
            P("col", None),
            P(),
        ),
        out_specs=(P("col", "row"), P(None, "col", None, "row")),
        check_vma=False,
    )
```

```python
import functools

import jax
import jax.numpy as jnp
from jax import lax
from jax.experimental import pallas as pl
from jax.experimental.pallas import tpu as pltpu
from jax.sharding import PartitionSpec as P

HDIM = 64
PAGE = 16
BASE_MAX = 16
EPSILON = 1e-05
NEGATIVE = -1e30
CHUNKS = 4
MIB = 1 << 20
MESH = pl.DeviceIdType.MESH


def collect_kernel(
    n, minors, in_ref, out_ref, local_sem, send1, recv1, send2, recv2, send3, recv3
):
    majors, length = n // (2 * minors), in_ref.shape[1]
    me, side = lax.axis_index("col"), lax.axis_index("row")
    core, chip = me % 2, me // 2
    minor, major = chip % minors, chip // minors

    def device(k, m, c):
        return (((major + k) % majors) * minors + (minor + m) % minors) * 2 + c

    def slot(at):
        return out_ref.at[:, pl.ds(pl.multiple_of(at * length, length), length)]

    def copy(source, at, sends, recvs, target):
        return pltpu.make_async_remote_copy(
            src_ref=source,
            dst_ref=slot(at),
            send_sem=sends,
            recv_sem=recvs,
            device_id=(side, target),
            device_id_type=MESH,
        )

    peers = [device(k, 0, core) for k in range(1, majors)]
    peers += [device(0, m, core) for m in range(1, minors)]
    peers += [device(0, 0, 1 - core)]
    barrier = pltpu.get_barrier_semaphore()
    for peer in peers:
        pl.semaphore_signal(barrier, inc=1, device_id=(side, peer), device_id_type=MESH)
    pl.semaphore_wait(barrier, len(peers))

    first = [
        copy(in_ref, me, send1.at[k], recv1.at[k], device(k, 0, core)) for k in range(1, majors)
    ]
    for each in first:
        each.start()
    own = pltpu.make_async_copy(in_ref, slot(me), local_sem)
    own.start()
    second, third = {}, []
    for k in range(majors):
        at = device(majors - k, 0, core)
        if k:
            first[k - 1].wait_recv()
        source = slot(at) if k else in_ref
        for m in range(1, minors):
            each = copy(source, at, send2.at[k, m], recv2.at[k, m], device(0, m, core))
            each.start()
            second[k, m] = each
        each = copy(source, at, send3.at[k, 0], recv3.at[k, 0], device(0, 0, 1 - core))
        each.start()
        third.append(each)
    for k in range(majors):
        for m in range(1, minors):
            at = device(majors - k, minors - m, core)
            second[k, m].wait_recv()
            each = copy(slot(at), at, send3.at[k, m], recv3.at[k, m], device(0, 0, 1 - core))
            each.start()
            third.append(each)
    own.wait()
    for each in first:
        each.wait_send()
    for each in second.values():
        each.wait_send()
    for each in third:
        each.wait()


def collect(value):
    n = lax.axis_size("col")
    minors = n // 8
    kinds, length, width = value.shape
    dma = pltpu.SemaphoreType.DMA
    return pl.pallas_call(
        functools.partial(collect_kernel, n, minors),
        in_specs=[pl.BlockSpec(memory_space=pl.ANY)],
        out_specs=pl.BlockSpec(memory_space=pl.ANY),
        out_shape=jax.ShapeDtypeStruct((kinds, n * length, width), value.dtype),
        scratch_shapes=[dma(())] + [dma((4,))] * 2 + [dma((4, minors))] * 4,
        compiler_params=pltpu.CompilerParams(collective_id=2, has_side_effects=True),
        name="collect",
    )(value)


def project_kernel(x_ref, w_ref, bias_ref, scale_ref, out_ref):
    sums = jnp.dot(x_ref[...], w_ref[0], preferred_element_type=jnp.float32)
    out_ref[0] = ((sums + bias_ref[0]) * scale_ref[0]).astype(jnp.bfloat16)


def project(tokens, weight, bias, scale):
    count, depth = tokens.shape
    width = weight.shape[2]
    return pl.pallas_call(
        project_kernel,
        grid=(3,),
        in_specs=[
            pl.BlockSpec((count, depth), lambda i: (0, 0)),
            pl.BlockSpec((1, depth, width), lambda i: (i, 0, 0)),
            pl.BlockSpec((1, 1, width), lambda i: (i, 0, 0)),
            pl.BlockSpec((1, 1, width), lambda i: (i, 0, 0)),
        ],
        out_specs=pl.BlockSpec((1, count, width), lambda i: (i, 0, 0)),
        out_shape=jax.ShapeDtypeStruct((3, count, width), jnp.bfloat16),
        compiler_params=pltpu.CompilerParams(vmem_limit_bytes=40 * MIB),
        cost_estimate=pl.CostEstimate(
            flops=5 * 10**9, bytes_accessed=8 * MIB, transcendentals=0
        ),
        name="project",
    )(tokens, weight, bias, scale)


def attend_kernel(q_ref, k_ref, v_ref, seg_col_ref, seg_row_ref, out_ref):
    allowed = seg_col_ref[...] == seg_row_ref[...]
    parts = []
    for h in range(q_ref.shape[2] // HDIM):
        cols = slice(h * HDIM, (h + 1) * HDIM)
        scores = lax.dot_general(
            q_ref[0, :, cols],
            k_ref[0, :, cols],
            (((1,), (1,)), ((), ())),
            preferred_element_type=jnp.float32,
        )
        scores = jnp.where(allowed, scores, NEGATIVE)
        highest = jnp.max(scores, axis=1, keepdims=True)
        exponent = jnp.exp(scores - highest)
        total = jnp.sum(exponent, axis=1, keepdims=True)
        mixed = jnp.dot(
            exponent.astype(jnp.bfloat16), v_ref[0, :, cols], preferred_element_type=jnp.float32
        )
        parts.append(mixed / total)
    out_ref[...] = jnp.concatenate(parts, axis=1).astype(jnp.bfloat16)


def attention(qkv, seg_col, seg_row, chunk, rows):
    _, count, width = qkv.shape
    step = 256
    return pl.pallas_call(
        attend_kernel,
        grid=(width // step,),
        in_specs=[
            pl.BlockSpec((1, rows, step), lambda i: (0, chunk, i)),
            pl.BlockSpec((1, count, step), lambda i: (1, 0, i)),
            pl.BlockSpec((1, count, step), lambda i: (2, 0, i)),
            pl.BlockSpec((rows, 1), lambda i: (chunk, 0)),
            pl.BlockSpec((1, count), lambda i: (0, 0)),
        ],
        out_specs=pl.BlockSpec((rows, step), lambda i: (0, i)),
        out_shape=jax.ShapeDtypeStruct((rows, width), jnp.bfloat16),
        compiler_params=pltpu.CompilerParams(vmem_limit_bytes=40 * MIB),
        cost_estimate=pl.CostEstimate(
            flops=5 * 10**9, bytes_accessed=3 * MIB, transcendentals=2 * MIB
        ),
        name="attention",
    )(qkv, qkv, qkv, seg_col, seg_row)


def feed_kernel(
    side_ref, mine_ref, theirs_ref, x_ref, vec_ref, w_ref, bias_ref,
    *rest,
):
    *part_refs, half_ref, normed_ref, sum_ref = rest
    step = pl.program_id(0)
    width = half_ref.shape[1]
    count = len(part_refs)

    def columns(at):
        at = at % count
        return slice(at * width, (at + 1) * width)

    @pl.when(step == 0)
    def _():
        summed = (
            x_ref[...].astype(jnp.float32)
            + (mine_ref[...].astype(jnp.float32) + theirs_ref[...].astype(jnp.float32))
            + vec_ref[0:1]
        )
        average = jnp.mean(summed, axis=1, keepdims=True)
        variance = jnp.mean(summed * summed, axis=1, keepdims=True) - average * average
        normed = (summed - average) * lax.rsqrt(variance + EPSILON) * vec_ref[1:2] + vec_ref[2:3]
        normed_ref[...] = normed.astype(jnp.bfloat16)
        sum_ref[...] = jnp.zeros_like(sum_ref)

        for side in range(count):

            @pl.when(side_ref[0] == side)
            def _():
                half_ref[...] = normed_ref[:, columns(side)]

    hidden = jnp.dot(normed_ref[...], w_ref[0], preferred_element_type=jnp.float32)
    hidden = hidden + bias_ref[...]
    hidden = (0.5 * hidden * (1.0 + lax.erf(hidden * 0.5**0.5))).astype(jnp.bfloat16)
    sum_ref[...] += lax.dot_general(
        hidden, w_ref[1], (((1,), (1,)), ((), ())), preferred_element_type=jnp.float32
    )

    @pl.when(step == pl.num_programs(0) - 1)
    def _():
        for side in range(count):

            @pl.when(side_ref[0] == side)
            def _():
                for k, part_ref in enumerate(part_refs):
                    part_ref[...] = sum_ref[:, columns(side + k)].astype(jnp.bfloat16)


def feed(side, mine, theirs, tokens, chunk, vectors, weight, bias):
    rows, depth = mine.shape
    count = lax.axis_size("row")
    width = depth // count
    units = weight.shape[2]
    step = 512
    whole = pl.BlockSpec((rows, depth), lambda i, s: (0, 0))
    half = pl.BlockSpec((rows, width), lambda i, s: (0, 0))
    return pl.pallas_call(
        feed_kernel,
        grid_spec=pltpu.PrefetchScalarGridSpec(
            num_scalar_prefetch=1,
            grid=(units // step,),
            in_specs=[
                whole,
                whole,
                pl.BlockSpec((rows, depth), lambda i, s: (chunk, 0)),
                pl.BlockSpec((3, depth), lambda i, s: (0, 0)),
                pl.BlockSpec((2, depth, step), lambda i, s: (0, 0, i)),
                pl.BlockSpec((1, step), lambda i, s: (0, i)),
            ],
            out_specs=[half] * (count + 1),
            scratch_shapes=[
                pltpu.VMEM((rows, depth), jnp.bfloat16),
                pltpu.VMEM((rows, depth), jnp.float32),
            ],
        ),
        out_shape=[jax.ShapeDtypeStruct((rows, width), jnp.bfloat16)] * (count + 1),
        compiler_params=pltpu.CompilerParams(vmem_limit_bytes=40 * MIB),
        cost_estimate=pl.CostEstimate(
            flops=8 * 10**9, bytes_accessed=10 * MIB, transcendentals=rows * units
        ),
        name="feed",
    )(side, mine, theirs, tokens, vectors, weight, bias)


def dispatch_kernel(
    n, sides, out_ref, got_ref, local_sem, send_sem, recv_sem, send2_sem, recv2_sem
):
    me, side = lax.axis_index("col"), lax.axis_index("row")
    barrier = pltpu.get_barrier_semaphore()
    for k in range(1, n):
        pl.semaphore_signal(
            barrier, inc=1, device_id=(side, lax.rem(me + k, n)), device_id_type=MESH
        )
    for j in range(1, sides):
        pl.semaphore_signal(
            barrier, inc=1, device_id=(lax.rem(side + j, sides), me), device_id_type=MESH
        )
    pl.semaphore_wait(barrier, n - 1 + sides - 1)

    def first(k):
        target = lax.rem(me + k, n)
        return pltpu.make_async_remote_copy(
            src_ref=out_ref.at[target],
            dst_ref=got_ref.at[side, me],
            send_sem=send_sem.at[k],
            recv_sem=recv_sem.at[k],
            device_id=(side, target),
            device_id_type=MESH,
        )

    def second(j, k, source):
        return pltpu.make_async_remote_copy(
            src_ref=source,
            dst_ref=got_ref.at[side, lax.rem(me + n - k, n)],
            send_sem=send2_sem.at[j, k],
            recv_sem=recv2_sem.at[j, k],
            device_id=(lax.rem(side + j, sides), me),
            device_id_type=MESH,
        )

    firsts = [first(k) for k in range(1, n)]
    for copy in firsts:
        copy.start()
    own = pltpu.make_async_copy(out_ref.at[me], got_ref.at[side, me], local_sem)
    own.start()
    seconds = [second(j, 0, out_ref.at[me]) for j in range(1, sides)]
    for copy in seconds:
        copy.start()
    for k in range(1, n):
        firsts[k - 1].wait_recv()
        for j in range(1, sides):
            copy = second(j, k, got_ref.at[side, lax.rem(me + n - k, n)])
            copy.start()
            seconds.append(copy)
    own.wait()
    for copy in firsts:
        copy.wait_send()
    for copy in seconds:
        copy.wait()


def dispatch(outgoing):
    n, rows, width = outgoing.shape
    sides = lax.axis_size("row")
    return pl.pallas_call(
        functools.partial(dispatch_kernel, n, sides),
        in_specs=[pl.BlockSpec(memory_space=pl.ANY)],
        out_specs=pl.BlockSpec(memory_space=pl.ANY),
        out_shape=jax.ShapeDtypeStruct((sides, n, rows, width), outgoing.dtype),
        scratch_shapes=[pltpu.SemaphoreType.DMA(())]
        + [pltpu.SemaphoreType.DMA((n,))] * 2
        + [pltpu.SemaphoreType.DMA((sides, n))] * 2,
        compiler_params=pltpu.CompilerParams(collective_id=1, has_side_effects=True),
        name="dispatch",
    )(outgoing)


def cache_kernel(index_ref, got_ref, w_ref, out_ref, x_ref, *, pages):
    base = pl.program_id(0) * pages
    half = got_ref.shape[2]
    for j in range(pages):
        at = index_ref[base + j]
        rows = pl.ds(pl.multiple_of(jnp.maximum(at, 0) * PAGE, PAGE), PAGE)
        for s in range(got_ref.shape[0]):
            page = got_ref[s, rows, :]
            page = jnp.where(at >= 0, page, jnp.zeros_like(page))
            x_ref[j * PAGE : (j + 1) * PAGE, s * half : (s + 1) * half] = page
    x = x_ref[...]
    for d in range(w_ref.shape[0]):
        pair = [
            jnp.dot(x, w_ref[d, k], preferred_element_type=jnp.float32).astype(jnp.bfloat16)
            for k in range(2)
        ]
        out_ref[d] = jnp.stack(pair, axis=1)


def fill_cache(index, got, weight, pages):
    own_pages = index.shape[0]
    layers, _, depth, width = weight.shape
    return pl.pallas_call(
        functools.partial(cache_kernel, pages=pages),
        grid_spec=pltpu.PrefetchScalarGridSpec(
            num_scalar_prefetch=1,
            grid=(own_pages // pages,),
            in_specs=[
                pl.BlockSpec(got.shape, lambda i, s: (0, 0, 0)),
                pl.BlockSpec(weight.shape, lambda i, s: (0, 0, 0, 0)),
            ],
            out_specs=pl.BlockSpec((layers, pages * PAGE, 2, width), lambda i, s: (0, i, 0, 0)),
            scratch_shapes=[pltpu.VMEM((pages * PAGE, depth), jnp.bfloat16)],
        ),
        out_shape=jax.ShapeDtypeStruct((layers, own_pages * PAGE, 2, width), jnp.bfloat16),
        compiler_params=pltpu.CompilerParams(vmem_limit_bytes=40 * MIB),
        cost_estimate=pl.CostEstimate(
            flops=10**10, bytes_accessed=18 * MIB, transcendentals=0
        ),
        name="fill_cache",
    )(index, got, weight)


def send(value, step):
    count = lax.axis_size("row")
    return lax.ppermute(value, "row", [(i, (i + step) % count) for i in range(count)])


def from_others(values):
    got = [send(value, k + 1) for k, value in enumerate(values)]
    if len(got) == 1:
        return got[0]
    return sum(value.astype(jnp.float32) for value in got)


def times_transposed(left, right):
    return lax.dot_general(
        left, right, (((1,), (1,)), ((), ())), preferred_element_type=jnp.float32
    )


def per_device(
    tokens,
    segment_ids,
    qkv_weight,
    attn_bias,
    out_weight,
    ffn_in,
    ffn_bias,
    ffn_out,
    norm_gain,
    shift,
    cross_weight,
    page_owner,
    cache_base,
):
    token_count = tokens.shape[0]
    n, me = lax.axis_size("col"), lax.axis_index("col")

    def gather(value, axis):
        return lax.all_gather(value, "col", axis=axis, tiled=True)

    w_first = collect(
        jnp.concatenate([qkv_weight[0].transpose(1, 0, 2), out_weight.transpose(0, 2, 1)])
    )
    w_ffn = gather(jnp.concatenate([ffn_in, ffn_out.transpose(0, 2, 1)]), 1)
    w_cross = gather(cross_weight.transpose(0, 2, 1, 3), 2)
    all_owners = lax.all_gather(page_owner[:, 0], "col")

    page_count = page_owner.shape[0]
    capacity = max(2, (2 * page_count + n - 1) // n)
    owner_ids = jnp.arange(n, dtype=jnp.int32)
    owners = page_owner[:, 0]
    onehot = (owners[:, None] == owner_ids[None, :]).astype(jnp.int32)
    local_rank = jnp.sum((jnp.cumsum(onehot, axis=0) - onehot) * onehot, axis=1)
    target = owners * capacity + local_rank
    token_target = (
        target[:, None] * PAGE + jnp.arange(PAGE, dtype=jnp.int32)[None, :]
    ).reshape(token_count)
    received = jnp.sum((all_owners == me).astype(jnp.int32), axis=1)
    earlier = jnp.cumsum(received) - received
    own_base = jnp.sum(jnp.where(owner_ids == me, cache_base, 0))
    place_ids = jnp.arange(capacity, dtype=jnp.int32)
    slots = jnp.where(
        place_ids[None, :] < received[:, None],
        own_base + earlier[:, None] + place_ids[None, :],
        -1,
    ).reshape(n * capacity)
    own_pages = BASE_MAX + capacity * n
    hits = jnp.arange(own_pages, dtype=jnp.int32)[:, None] == slots[None, :]
    page_at = jnp.max(
        jnp.where(hits, jnp.arange(n * capacity, dtype=jnp.int32)[None, :], -1), axis=1
    )

    page_at, token_target, tokens = lax.optimization_barrier((page_at, token_target, tokens))
    width = cross_weight.shape[3]
    side = lax.axis_index("row")
    others = lax.axis_size("row") - 1
    bias = jnp.stack([attn_bias[0, 0], jnp.zeros_like(attn_bias[0, 0]), attn_bias[0, 1]])
    scale = jnp.array([HDIM ** (-0.5), 1.0, 1.0], jnp.float32)[:, None, None]
    scale = jnp.broadcast_to(scale, (3, 1, bias.shape[1]))
    qkv = project(tokens, w_first, bias[:, None, :], scale)
    w_out = w_first[3]
    vectors = jnp.stack([shift[0, 0], norm_gain[0, 0], shift[0, 1]])
    rows = token_count // CHUNKS
    seg_col, seg_row = segment_ids[:, None], segment_ids[None, :]
    partials = []
    for c in range(CHUNKS):
        context = attention(qkv, seg_col, seg_row, c, rows)
        mine = times_transposed(context, w_out).astype(jnp.bfloat16)
        partials.append((mine, from_others([mine] * others)))
    kept, taken, halves = [], [], []
    for c, (mine, theirs) in enumerate(partials):
        keep, *sends, half = feed(
            side.reshape(1), mine, theirs, tokens, c, vectors, w_ffn, ffn_bias
        )
        kept.append(keep)
        taken.append(from_others(sends))
        halves.append(half)

    def own(row):
        return lax.dynamic_slice_in_dim(row, side * width, width, 0)

    summed = (
        jnp.concatenate(halves).astype(jnp.float32)
        + (jnp.concatenate(kept).astype(jnp.float32) + jnp.concatenate(taken).astype(jnp.float32))
        + own(shift[0, 2])
    )
    sums = jnp.stack([jnp.sum(summed, axis=1), jnp.sum(summed * summed, axis=1)])
    moments = (sums + from_others([sums] * others)) / tokens.shape[1]
    average = moments[0][:, None]
    variance = moments[1][:, None] - average * average
    own_part = (
        (summed - average) * lax.rsqrt(variance + EPSILON) * own(norm_gain[0, 1])
        + own(shift[0, 3])
    ).astype(jnp.bfloat16)
    chosen = (
        jnp.arange(n * capacity * PAGE, dtype=jnp.int32)[:, None] == token_target[None, :]
    ).astype(jnp.bfloat16)
    outgoing = jnp.dot(chosen, own_part, preferred_element_type=jnp.float32)
    outgoing = outgoing.astype(jnp.bfloat16).reshape(n, capacity * PAGE, width)
    arrived = dispatch(outgoing).reshape(others + 1, n * capacity * PAGE, width)
    pages = 16 if own_pages % 16 == 0 else own_pages
    cache = fill_cache(page_at, arrived, w_cross, pages)
    return (own_part, cache)


def solution(mesh):
    return jax.shard_map(
        per_device,
        mesh=mesh,
        in_specs=(
            P("col", None),
            P("col"),
            P(None, "col", None, "row"),
            P(None, None, "row"),
            P(None, "row", "col"),
            P(None, "col", "row"),
            P(None, "row"),
            P(None, "row", "col"),
            P(),
            P(),
            P(None, "col", None, "row"),
            P("col", None),
            P(),
        ),
        out_specs=(P("col", "row"), P(None, "col", None, "row")),
        check_vma=False,
    )
```
